128 devices in a mesh: space: 8 (over x, z_lo), filt: 16 (over z_hi, y, core).
Axes of the slice: x: 4, y: 4, z: 4 (z_hi: 2, z_lo: 2; z = z_hi * 2 + z_lo), core: 2. Of those that a mesh axis runs over, the one named last changes fastest.
Arguments:
- layer_input: bfloat16 [32, 64, 32, 128], P('space', 'filt'), may hold values from -6 to 6
- first_kernel: bfloat16 [256, 3456], replicated, may hold values from -0.109375 to 0.109375
- second_kernel: bfloat16 [512, 6912], replicated, may hold values from -0.078125 to 0.078125
- cotangent: bfloat16 [512, 16, 512], P('filt', 'space'), may hold values from -0.29882812 to 0.29882812
Outputs:
- activation: float32 [512, 16, 512], P('filt', 'space')
- kernel_grad: float32 [256, 3456], P(('space', 'filt'))
The draws below stay inside these ranges and needn't reach their ends.
All inputs are finite; a program needn't handle non-finite values.
Results may differ from the reference program's by a relative error of at most 0.0055.
Values may be sent and summed in bfloat16 or wider, within the bound.
No kernel may reach another device: no remote copies, remote signals or barrier semaphores. Data moves between devices by JAX's collectives and lax.ppermute only.
A program may use at most 64 MiB of HBM per device.

```python
import jax
import jax.numpy as jnp
from jax import lax

CIN = 128
CMID = 256
COUT = 512
NZ = 32
NX = 32
NY = 64


def levels(own_key, extent, split, smallest, largest):
    def one(axis_at, blocks):
        steps = jax.random.uniform(jax.random.fold_in(jax.random.fold_in(own_key, 6), axis_at), (blocks,), jnp.float32, smallest / len(split), largest / len(split))
        return jnp.repeat(jnp.exp(steps), extent[axis_at] // blocks).reshape((-1,) + (1,) * (len(extent) - axis_at - 1))

    level = one(*split[0])
    for cut in split[1:]:
        level = level * one(*cut)
    return level


def normal_values(key, shape, scale, reach, pieces=(), held_as=jnp.bfloat16):
    loudness = levels(key, shape, pieces, -0.22, 0.18) if pieces else 1.0
    values = jax.random.normal(key, shape, jnp.float32) * scale * loudness
    return jnp.minimum(jnp.maximum(values, -reach), reach).astype(held_as)


def setup_inputs(seed: int = 0) -> dict:
    key_list = jax.random.split(jax.random.key(seed), 5)
    layer_input = normal_values(key_list[0], (NX, NY, NZ, CIN), 1.0, 6.0, ((0, 8), (1, 16)))
    first_kernel = normal_values(key_list[1], (CMID, 27 * CIN), (27 * CIN) ** -0.5, 0.109375)
    second_kernel = normal_values(key_list[2], (COUT, 27 * CMID), (27 * CMID) ** -0.5, 0.078125)
    cotangent = normal_values(key_list[3], (COUT, NX // 2, (NY // 2) * (NZ // 2)), 0.05, 0.29882812, ((0, 16), (1, 8)))
    return dict(layer_input=layer_input, first_kernel=first_kernel, second_kernel=second_kernel, cotangent=cotangent)


def silu_slope(values):
    logistic = jax.nn.sigmoid(values)
    return logistic * (1.0 + values * (1.0 - logistic))


def correlate(field, kernel):
    result = lax.conv_general_dilated(field[None], kernel, (1, 1, 1), "SAME", dimension_numbers=("NDHWC", "DHWIO", "NDHWC"), precision=lax.Precision.HIGHEST, preferred_element_type=jnp.float32)
    return result[0]


def reference(layer_input, first_kernel, second_kernel, cotangent):
    kernel_one = first_kernel.astype(jnp.float32).reshape(CMID, 3, 3, 3, CIN).transpose(1, 2, 3, 4, 0)
    pre_first = correlate(layer_input.astype(jnp.float32), kernel_one)
    pooled = (jax.nn.silu(pre_first).reshape(NX // 2, 2, NY // 2, 2, NZ // 2, 2, CMID).sum(axis=(1, 3, 5)) * 0.125).astype(jnp.bfloat16)
    kernel_two = second_kernel.astype(jnp.float32).reshape(COUT, 3, 3, 3, CMID).transpose(1, 2, 3, 4, 0)
    pre_second = correlate(pooled.astype(jnp.float32), kernel_two).transpose(3, 0, 1, 2).reshape(COUT, NX // 2, (NY // 2) * (NZ // 2))
    activation = jax.nn.silu(pre_second)
    grad_second = (cotangent.astype(jnp.float32) * silu_slope(pre_second)).astype(jnp.bfloat16)
    grad_field = grad_second.astype(jnp.float32).reshape(COUT, NX // 2, NY // 2, NZ // 2).transpose(1, 2, 3, 0)
    flipped = second_kernel.astype(jnp.float32).reshape(COUT, 3, 3, 3, CMID)[:, ::-1, ::-1, ::-1, :].transpose(1, 2, 3, 0, 4)
    pooled_grad = correlate(grad_field, flipped)
    spread = jnp.broadcast_to(pooled_grad[:, None, :, None, :, None, :], (NX // 2, 2, NY // 2, 2, NZ // 2, 2, CMID)).reshape(NX, NY, NZ, CMID) * 0.125
    grad_first = spread * silu_slope(pre_first)
    flat_grad = grad_first.reshape(-1, CMID)
    padded_in = jnp.pad(layer_input.astype(jnp.float32), ((1, 1), (1, 1), (1, 1), (0, 0)))
    blocks = []
    for along_x in (-1, 0, 1):
        for along_y in (-1, 0, 1):
            for along_z in (-1, 0, 1):
                tap_slice = lax.slice(padded_in, (1 + along_x, 1 + along_y, 1 + along_z, 0), (1 + along_x + NX, 1 + along_y + NY, 1 + along_z + NZ, CIN)).reshape(-1, CIN)
                blocks.append(lax.dot_general(flat_grad, tap_slice, (((0,), (0,)), ((), ())), precision=lax.Precision.HIGHEST, preferred_element_type=jnp.float32))
    return activation, jnp.concatenate(blocks, axis=1)
```

```python
import jax
import jax.numpy as jnp
from jax import lax
from jax.experimental import pallas as pl
from jax.experimental.pallas import tpu as pltpu
from jax.sharding import PartitionSpec as P

BOTH = ("space", "filt")
F32 = jnp.float32
BF16 = jnp.bfloat16
VMEM = pl.BlockSpec(memory_space=pltpu.VMEM)
HBM = pl.BlockSpec(memory_space=pl.ANY)


def nt(left, right):
    return lax.dot_general(left, right, (((1,), (1,)), ((), ())), preferred_element_type=F32)


def nn(left, right):
    return lax.dot_general(left, right, (((1,), (0,)), ((), ())), preferred_element_type=F32)


def sigmoid(v):
    return 1.0 / (1.0 + jnp.exp(-v))


def shifted(v, step):
    rows = v.shape[1]
    wide = v.astype(F32)
    at = lax.broadcasted_iota(jnp.int32, wide.shape, 1)
    moved = pltpu.roll(wide, (-step) % rows, 1)
    edge = rows - 1 if step > 0 else 0
    return jnp.where(at == edge, 0.0, moved).astype(BF16)


def forward_kernel(own, xm, xp, off, dm, dp, pair, w1, cot, w2_hbm, xc_out, slope_out, act_out, g2_out, xc, pc, w2, sem):
    load = pltpu.make_async_copy(w2_hbm, w2, sem)
    load.start()
    space_at = lax.axis_index("space")
    filt_at = lax.axis_index("filt")
    parity = lax.rem(filt_at, 2)
    off_y = parity * 7
    pair_y = 7 - parity * 7

    def put(piece, x0, y0):
        nx, ny = piece.shape[:2]
        v = piece[...].reshape(nx * ny, 16, 256)
        even, odd = v[:, :, :128], v[:, :, 128:]
        where = (pl.ds(x0, nx), pl.ds(y0, ny))
        shape = (nx, ny, 16, 128)
        xc[where + (slice(None), slice(0, 128))] = shifted(odd, -1).reshape(shape)
        xc[where + (slice(None), slice(128, 256))] = even.reshape(shape)
        xc[where + (slice(None), slice(256, 384))] = odd.reshape(shape)
        xc[where + (slice(None), slice(384, 512))] = shifted(even, 1).reshape(shape)

    put(own, 3, 3)
    put(xm, 0, 3)
    put(xp, 7, 3)
    put(off, 3, off_y)
    put(dm, 0, off_y)
    put(dp, 7, off_y)
    put(pair, 0, pair_y)
    xc_out[...] = xc[2:8, 2:8]

    for plane in range(4):
        total = None
        for r in range(2):
            pre = None
            for a in range(3):
                lhs = jnp.concatenate(
                    [
                        xc[2 * plane + a : 2 * plane + a + 2, b : b + 8, :, r * 128 : r * 128 + 384].reshape(256, 384)
                        for b in range(3)
                    ],
                    axis=1,
                )
                part = nt(lhs, w1[:, a * 1152 : (a + 1) * 1152])
                pre = part if pre is None else pre + part
            pre = pre.reshape(2, 8, 16, 256)
            logistic = sigmoid(pre)
            if plane in (1, 2):
                inner, gate = pre[:, 2:6], logistic[:, 2:6]
                slope_out[r, 2 * plane - 2 : 2 * plane] = gate * (1.0 + inner * (1.0 - gate))
            value = (pre * logistic).reshape(2, 4, 2, 16, 256)
            value = (value[0, :, 0] + value[0, :, 1]) + (value[1, :, 0] + value[1, :, 1])
            total = value if total is None else total + value
        row = lax.broadcasted_iota(jnp.int32, total.shape, 0)
        keep = ((row > 0) | (filt_at > 0)) & ((row < 3) | (filt_at < 15))
        if plane == 0:
            keep = keep & (space_at > 0)
        if plane == 3:
            keep = keep & (space_at < 7)
        pooled = jnp.where(keep, total * 0.125, 0.0).astype(BF16)
        pc[plane, :, :, 0:256] = shifted(pooled, -1)
        pc[plane, :, :, 256:512] = pooled
        pc[plane, :, :, 512:768] = shifted(pooled, 1)

    load.wait()
    pre = None
    for a in range(3):
        for b in range(3):
            t = 3 * a + b
            cells = pc[a : a + 2, b : b + 2].reshape(64, 768)
            part = nt(w2[:, t * 768 : (t + 1) * 768], cells)
            pre = part if pre is None else pre + part
    logistic = sigmoid(pre)
    act_out[...] = (pre * logistic).astype(act_out.dtype)
    grad = cot[...].astype(F32) * (logistic * (1.0 + pre * (1.0 - logistic)))
    g2_out[...] = jnp.transpose(grad).astype(BF16).reshape(2, 2, 16, 512)


def backward_kernel(own, xm, xp, off, dm, dp, pair, slope, xc, w2_hbm, keep_out, send_out, gc, w2, sem):
    loads = []
    for t in range(9):
        lanes = slice(t * 768, (t + 1) * 768)
        loads.append(pltpu.make_async_copy(w2_hbm.at[:, lanes], w2.at[:, lanes], sem.at[t]))
        loads[-1].start()
    parity = lax.rem(lax.axis_index("filt"), 2)
    off_y = parity * 3
    pair_y = 3 - parity * 3

    def put(piece, x0, y0):
        nx, ny = piece.shape[:2]
        v = piece[...].reshape(nx * ny, 16, 512)
        where = (pl.ds(x0, nx), pl.ds(y0, ny))
        shape = (nx, ny, 16, 512)
        gc[where + (slice(None), slice(0, 512))] = shifted(v, 1).reshape(shape)
        gc[where + (slice(None), slice(512, 1024))] = v.reshape(shape)
        gc[where + (slice(None), slice(1024, 1536))] = shifted(v, -1).reshape(shape)

    put(own, 1, 1)
    put(xm, 0, 1)
    put(xp, 3, 1)
    put(off, 1, off_y)
    put(dm, 0, off_y)
    put(dp, 3, off_y)
    put(pair, 0, pair_y)

    acc = None
    for a in range(3):
        for b in range(3):
            t = 3 * a + b
            loads[t].wait()
            for c in range(3):
                cells = gc[2 - a : 4 - a, 2 - b : 4 - b, :, c * 512 : (c + 1) * 512].reshape(64, 512)
                part = nn(cells, w2[:, (3 * t + c) * 256 : (3 * t + c + 1) * 256])
                acc = part if acc is None else acc + part
    acc = (acc * 0.125).reshape(2, 2, 16, 256)

    row = lax.broadcasted_iota(jnp.int32, (256, 256), 0)
    column = lax.broadcasted_iota(jnp.int32, (256, 256), 1)
    half = row // 128
    inside = row - half * 128
    want = 4 * (inside // 2) + lax.rem(inside, 2) + 2 * jnp.where(half == 0, parity, 1 - parity)
    order = jnp.where(column == want, 1.0, 0.0).astype(BF16)
    turned = []
    for r in range(2):
        grads = [
            (acc[x // 2, y // 2] * slope[r, x, y]).astype(BF16)
            for x in range(4)
            for y in range(4)
        ]
        turned.append(nt(order, jnp.concatenate(grads, axis=0)).astype(BF16))
    for a in range(3):
        for b in range(3):
            t = 3 * a + b
            part = None
            for r in range(2):
                cells = xc[a : a + 4, b : b + 4, :, r * 128 : r * 128 + 384].reshape(256, 384)
                one = nn(turned[r], cells)
                part = one if part is None else part + one
            part = part.astype(BF16)
            keep_out[:, t * 384 : (t + 1) * 384] = part[:128]
            send_out[:, t * 384 : (t + 1) * 384] = part[128:]


def route(step, across, spaces, filts):
    pairs = []
    for i in range(spaces):
        for j in range(filts):
            to_i = i + step
            to_j = (j + 1 if j % 2 else j - 1) if across else j
            if 0 <= to_i < spaces and 0 <= to_j < filts:
                pairs.append((i * filts + j, to_i * filts + to_j))
    return pairs


def surround(x, width):
    spaces, filts = lax.axis_size("space"), lax.axis_size("filt")
    length = x.shape[1]
    parity = lax.rem(lax.axis_index("filt"), 2)
    far = parity * (length - width)
    near = (length - width) - far
    last, first = x[x.shape[0] - width :], x[:width]
    xm = lax.ppermute(last, BOTH, route(1, False, spaces, filts))
    xp = lax.ppermute(first, BOTH, route(-1, False, spaces, filts))
    rows = lax.dynamic_slice_in_dim(x, far, width, 1)
    off = lax.ppermute(rows, BOTH, route(0, True, spaces, filts))
    dm = lax.ppermute(rows[x.shape[0] - width :], BOTH, route(1, True, spaces, filts))
    dp = lax.ppermute(rows[:width], BOTH, route(-1, True, spaces, filts))
    mine = lax.dynamic_slice_in_dim(jnp.concatenate([xm, x, xp], axis=0), near, width, 1)
    pair = lax.ppermute(mine, "filt", [(j, j ^ 1) for j in range(filts)])
    return x, xm, xp, off, dm, dp, pair


def local(layer_input, first_kernel, second_kernel, cotangent):
    filts = lax.axis_size("filt")
    folded = layer_input.reshape(4, 4, 16, 256)
    pieces = surround(folded, 3)
    cot = cotangent.reshape(32, 2, 16, 32).transpose(2, 0, 1, 3).reshape(16, 2048)
    cot = lax.all_to_all(cot, "filt", 0, 0, tiled=True).reshape(512, 64)
    xc, slope, act, grad = pl.pallas_call(
        forward_kernel,
        out_shape=(
            jax.ShapeDtypeStruct((6, 6, 16, 512), BF16),
            jax.ShapeDtypeStruct((2, 4, 4, 16, 256), F32),
            jax.ShapeDtypeStruct((512, 64), F32),
            jax.ShapeDtypeStruct((2, 2, 16, 512), BF16),
        ),
        in_specs=[VMEM] * 9 + [HBM],
        out_specs=(VMEM,) * 4,
        scratch_shapes=[
            pltpu.VMEM((10, 10, 16, 512), BF16),
            pltpu.VMEM((4, 4, 16, 768), BF16),
            pltpu.VMEM((512, 6912), BF16),
            pltpu.SemaphoreType.DMA,
        ],
        name="forward_layers",
    )(*pieces, first_kernel, cot, second_kernel)
    grads = surround(grad, 1)
    act = lax.all_to_all(act.astype(BF16).reshape(16, 2048), "filt", 0, 0, tiled=True)
    activation = act.reshape(16, 32, 2, 32).transpose(1, 2, 0, 3).reshape(32, 2, 512).astype(F32)
    keep, send = pl.pallas_call(
        backward_kernel,
        out_shape=(jax.ShapeDtypeStruct((128, 3456), BF16),) * 2,
        in_specs=[VMEM] * 9 + [HBM],
        out_specs=(VMEM,) * 2,
        scratch_shapes=[
            pltpu.VMEM((4, 4, 16, 1536), BF16),
            pltpu.VMEM((512, 6912), BF16),
            pltpu.SemaphoreType.DMA((9,)),
        ],
        name="backward_layers",
    )(*grads, slope, xc, second_kernel)
    got = lax.ppermute(send, "filt", [(j, j ^ 1) for j in range(filts)])
    both = (keep.astype(F32) + got.astype(F32)).astype(BF16)
    spaces = lax.axis_size("space")
    groups = [[i * filts + j for i in range(spaces) for j in range(c, filts, 2)] for c in range(2)]
    parts = lax.all_to_all(both, BOTH, 0, 0, axis_index_groups=groups, tiled=True)
    kernel_grad = parts.reshape(64, 2, 3456).astype(F32).sum(axis=0)
    return (activation, kernel_grad)


def solution(mesh):
    return jax.shard_map(
        local,
        mesh=mesh,
        in_specs=(P("space", "filt", None, None), P(), P(), P("filt", "space", None)),
        out_specs=(P("filt", "space", None), P(BOTH, None)),
        check_vma=False,
    )
```

```python
import jax
import jax.numpy as jnp
from jax import lax
from jax.experimental import pallas as pl
from jax.experimental.pallas import tpu as pltpu
from jax.sharding import PartitionSpec as P


BOTH = ("space", "filt")
F32 = jnp.float32
BF16 = jnp.bfloat16
VMEM = pl.BlockSpec(memory_space=pltpu.VMEM)
HBM = pl.BlockSpec(memory_space=pltpu.HBM)


def nt(left, right):
    return lax.dot_general(left, right, (((1,), (1,)), ((), ())), preferred_element_type=F32)


def nn(left, right):
    return lax.dot_general(left, right, (((1,), (0,)), ((), ())), preferred_element_type=F32)


def sigmoid(v):
    return 1.0 / (1.0 + jnp.exp(-v))


def shifted(v, step):
    rows = v.shape[1]
    wide = v.astype(F32)
    at = lax.broadcasted_iota(jnp.int32, wide.shape, 1)
    moved = pltpu.roll(wide, (-step) % rows, 1)
    edge = rows - 1 if step > 0 else 0
    return jnp.where(at == edge, 0.0, moved).astype(BF16)


def first_kernel_body(own, xm, xp, off, pair, w1, xc_out, slope_out, pooled_out, xc):
    space_at = lax.axis_index("space")
    filt_at = lax.axis_index("filt")
    parity = lax.rem(filt_at, 2)
    off_y = parity * 7
    pair_y = 7 - parity * 7

    def put(piece, x0, y0):
        nx, ny = piece.shape[:2]
        v = piece[...].reshape(nx * ny, 16, 256)
        even, odd = v[:, :, :128], v[:, :, 128:]
        where = (pl.ds(x0, nx), pl.ds(y0, ny))
        shape = (nx, ny, 16, 128)
        xc[where + (slice(None), slice(0, 128))] = shifted(odd, -1).reshape(shape)
        xc[where + (slice(None), slice(128, 256))] = even.reshape(shape)
        xc[where + (slice(None), slice(256, 384))] = odd.reshape(shape)
        xc[where + (slice(None), slice(384, 512))] = shifted(even, 1).reshape(shape)

    put(own, 3, 3)
    put(xm, 0, 3)
    put(xp, 7, 3)
    put(off, 0, off_y)
    put(pair, 0, pair_y)
    xc_out[...] = xc[2:8, 2:8]

    for plane in range(4):
        total = None
        for r in range(2):
            pre = None
            for a in range(3):
                lhs = jnp.concatenate(
                    [
                        xc[2 * plane + a : 2 * plane + a + 2, b : b + 8, :, r * 128 : r * 128 + 384].reshape(256, 384)
                        for b in range(3)
                    ],
                    axis=1,
                )
                part = nt(lhs, w1[:, a * 1152 : (a + 1) * 1152])
                pre = part if pre is None else pre + part
            pre = pre.reshape(2, 8, 16, 256)
            logistic = sigmoid(pre)
            if plane in (1, 2):
                inner, gate = pre[:, 2:6], logistic[:, 2:6]
                slope_out[r, 2 * plane - 2 : 2 * plane] = gate * (1.0 + inner * (1.0 - gate))
            value = (pre * logistic).reshape(2, 4, 2, 16, 256)
            value = (value[0, :, 0] + value[0, :, 1]) + (value[1, :, 0] + value[1, :, 1])
            total = value if total is None else total + value
        row = lax.broadcasted_iota(jnp.int32, total.shape, 0)
        keep = ((row > 0) | (filt_at > 0)) & ((row < 3) | (filt_at < 15))
        if plane == 0:
            keep = keep & (space_at > 0)
        if plane == 3:
            keep = keep & (space_at < 7)
        pooled_out[plane] = jnp.where(keep, total * 0.125, 0.0).astype(BF16)


def load_chunks(w2_hbm, w2, sem):
    loads = []
    for t in range(9):
        lanes = slice(t * 768, (t + 1) * 768)
        loads.append(pltpu.make_async_copy(w2_hbm.at[:, lanes], w2.at[:, lanes], sem.at[t]))
        loads[-1].start()
    return loads


def second_kernel_body(pooled, cot, w2_hbm, act_out, g2_out, pc, w2, sem):
    loads = load_chunks(w2_hbm, w2, sem)
    v = pooled[...].reshape(16, 16, 256)
    pc[:, :, :, 0:256] = shifted(v, -1).reshape(4, 4, 16, 256)
    pc[:, :, :, 256:512] = pooled[...]
    pc[:, :, :, 512:768] = shifted(v, 1).reshape(4, 4, 16, 256)
    pre = None
    for a in range(3):
        for b in range(3):
            t = 3 * a + b
            loads[t].wait()
            cells = pc[a : a + 2, b : b + 2].reshape(64, 768)
            part = nt(w2[:, t * 768 : (t + 1) * 768], cells)
            pre = part if pre is None else pre + part
    logistic = sigmoid(pre)
    act_out[...] = (pre * logistic).astype(act_out.dtype)
    grad = cot[...].astype(F32) * (logistic * (1.0 + pre * (1.0 - logistic)))
    g2_out[...] = jnp.transpose(grad).astype(BF16).reshape(2, 2, 16, 512)


def backward_kernel(own, xm, xp, off, pair, slope, xc, w2_hbm, keep_out, send_out, gc, w2, sem):
    loads = load_chunks(w2_hbm, w2, sem)
    parity = lax.rem(lax.axis_index("filt"), 2)
    off_y = parity * 3
    pair_y = 3 - parity * 3

    def put(piece, x0, y0):
        nx, ny = piece.shape[:2]
        v = piece[...].reshape(nx * ny, 16, 512)
        where = (pl.ds(x0, nx), pl.ds(y0, ny))
        shape = (nx, ny, 16, 512)
        gc[where + (slice(None), slice(0, 512))] = shifted(v, 1).reshape(shape)
        gc[where + (slice(None), slice(512, 1024))] = v.reshape(shape)
        gc[where + (slice(None), slice(1024, 1536))] = shifted(v, -1).reshape(shape)

    put(own, 1, 1)
    put(xm, 0, 1)
    put(xp, 3, 1)
    put(off, 0, off_y)
    put(pair, 0, pair_y)

    acc = None
    for a in range(3):
        for b in range(3):
            t = 3 * a + b
            loads[t].wait()
            for c in range(3):
                cells = gc[2 - a : 4 - a, 2 - b : 4 - b, :, c * 512 : (c + 1) * 512].reshape(64, 512)
                part = nn(cells, w2[:, (3 * t + c) * 256 : (3 * t + c + 1) * 256])
                acc = part if acc is None else acc + part
    acc = (acc * 0.125).reshape(2, 2, 16, 256)

    row = lax.broadcasted_iota(jnp.int32, (256, 256), 0)
    column = lax.broadcasted_iota(jnp.int32, (256, 256), 1)
    half = row // 128
    inside = row - half * 128
    want = 4 * (inside // 2) + lax.rem(inside, 2) + 2 * jnp.where(half == 0, parity, 1 - parity)
    order = jnp.where(column == want, 1.0, 0.0).astype(BF16)
    turned = []
    for r in range(2):
        grads = [
            (acc[x // 2, y // 2] * slope[r, x, y]).astype(BF16)
            for x in range(4)
            for y in range(4)
        ]
        turned.append(nt(order, jnp.concatenate(grads, axis=0)).astype(BF16))
    for a in range(3):
        for b in range(3):
            t = 3 * a + b
            part = None
            for r in range(2):
                cells = xc[a : a + 4, b : b + 4, :, r * 128 : r * 128 + 384].reshape(256, 384)
                one = nn(turned[r], cells)
                part = one if part is None else part + one
            part = part.astype(BF16)
            keep_out[:, t * 384 : (t + 1) * 384] = part[:128]
            send_out[:, t * 384 : (t + 1) * 384] = part[128:]


def route(step, across, spaces, filts):
    pairs = []
    for i in range(spaces):
        for j in range(filts):
            to_i = i + step
            to_j = (j + 1 if j % 2 else j - 1) if across else j
            if 0 <= to_i < spaces and 0 <= to_j < filts:
                pairs.append((i * filts + j, to_i * filts + to_j))
    return pairs


def surround(x, width):
    spaces, filts = lax.axis_size("space"), lax.axis_size("filt")
    length = x.shape[1]
    parity = lax.rem(lax.axis_index("filt"), 2)
    far = parity * (length - width)
    near = (length - width) - far
    last, first = x[x.shape[0] - width :], x[:width]
    xm = lax.ppermute(last, BOTH, route(1, False, spaces, filts))
    xp = lax.ppermute(first, BOTH, route(-1, False, spaces, filts))
    wide = jnp.concatenate([xm, x, xp], axis=0)
    off = lax.ppermute(lax.dynamic_slice_in_dim(wide, far, width, 1), BOTH, route(0, True, spaces, filts))
    pair = lax.ppermute(lax.dynamic_slice_in_dim(wide, near, width, 1), "filt", [(j, j ^ 1) for j in range(filts)])
    return x, xm, xp, off, pair


def steps(layer_input, first_kernel, second_kernel, cotangent):
    filts = lax.axis_size("filt")
    folded = layer_input.reshape(4, 4, 16, 256)
    pieces = surround(folded, 3)
    cot = cotangent.reshape(32, 2, 16, 32).transpose(2, 0, 1, 3).reshape(16, 16, 128)
    cot = lax.all_to_all(cot, "filt", 0, 0)
    cot = cot.reshape(512, 64)
    xc, slope, pooled = pl.pallas_call(
        first_kernel_body,
        out_shape=(
            jax.ShapeDtypeStruct((6, 6, 16, 512), BF16),
            jax.ShapeDtypeStruct((2, 4, 4, 16, 256), F32),
            jax.ShapeDtypeStruct((4, 4, 16, 256), BF16),
        ),
        in_specs=[VMEM] * 6,
        out_specs=(VMEM,) * 3,
        scratch_shapes=[pltpu.VMEM((10, 10, 16, 512), BF16)],
        compiler_params=pltpu.CompilerParams(vmem_limit_bytes=28 << 20),
        name="first_layer",
    )(*pieces, first_kernel)
    act, grad = pl.pallas_call(
        second_kernel_body,
        out_shape=(
            jax.ShapeDtypeStruct((512, 64), BF16),
            jax.ShapeDtypeStruct((2, 2, 16, 512), BF16),
        ),
        in_specs=[VMEM] * 2 + [HBM],
        out_specs=(VMEM,) * 2,
        scratch_shapes=[
            pltpu.VMEM((4, 4, 16, 768), BF16),
            pltpu.VMEM((512, 6912), BF16),
            pltpu.SemaphoreType.DMA((9,)),
        ],
        compiler_params=pltpu.CompilerParams(vmem_limit_bytes=28 << 20),
        name="second_layer",
    )(pooled, cot, second_kernel)
    grads = surround(grad, 1)
    keep, send = pl.pallas_call(
        backward_kernel,
        out_shape=(jax.ShapeDtypeStruct((128, 3456), BF16),) * 2,
        in_specs=[VMEM] * 7 + [HBM],
        out_specs=(VMEM,) * 2,
        scratch_shapes=[
            pltpu.VMEM((4, 4, 16, 1536), BF16),
            pltpu.VMEM((512, 6912), BF16),
            pltpu.SemaphoreType.DMA((9,)),
        ],
        compiler_params=pltpu.CompilerParams(vmem_limit_bytes=28 << 20),
        name="backward_layers",
    )(*grads, slope, xc, second_kernel)
    got = lax.ppermute(send, "filt", [(j, j ^ 1) for j in range(filts)])
    both = (keep.astype(F32) + got.astype(F32)).astype(BF16)
    spaces = lax.axis_size("space")
    groups = [[i * filts + j for i in range(spaces) for j in range(c, filts, 2)] for c in range(2)]
    parts = lax.all_to_all(both.reshape(64, 2, 3456), BOTH, 0, 0, axis_index_groups=groups)
    act = lax.all_to_all(act.reshape(16, 16, 128), "filt", 0, 0)
    activation = act.reshape(16, 32, 2, 32).transpose(1, 2, 0, 3).reshape(32, 2, 512).astype(F32)
    kernel_grad = parts.astype(F32).sum(axis=0)
    return (activation, kernel_grad)


def solution(mesh):
    return jax.shard_map(
        steps,
        mesh=mesh,
        in_specs=(P("space", "filt", None, None), P(), P(), P("filt", "space", None)),
        out_specs=(P("filt", "space", None), P(BOTH, None)),
        check_vma=False,
    )
```

```python
import jax
import jax.numpy as jnp
from jax import lax
from jax.experimental import pallas as pl
from jax.experimental.pallas import tpu as pltpu
from jax.sharding import PartitionSpec as P


BOTH = ("space", "filt")
F32 = jnp.float32
BF16 = jnp.bfloat16
VMEM = pl.BlockSpec(memory_space=pltpu.VMEM)
HBM = pl.BlockSpec(memory_space=pltpu.HBM)


def nt(left, right):
    return lax.dot_general(left, right, (((1,), (1,)), ((), ())), preferred_element_type=F32)


def nn(left, right):
    return lax.dot_general(left, right, (((1,), (0,)), ((), ())), preferred_element_type=F32)


def sigmoid(v):
    return 1.0 / (1.0 + jnp.exp(-v))


def shifted(v, step):
    rows = v.shape[1]
    wide = v.astype(F32)
    at = lax.broadcasted_iota(jnp.int32, wide.shape, 1)
    moved = pltpu.roll(wide, (-step) % rows, 1)
    edge = rows - 1 if step > 0 else 0
    return jnp.where(at == edge, 0.0, moved).astype(BF16)


def first_kernel_body(own, xm, xp, off, pair, w1, xc_out, slope_out, pooled_out, xc):
    space_at = lax.axis_index("space")
    filt_at = lax.axis_index("filt")
    parity = lax.rem(filt_at, 2)
    off_y = parity * 7
    pair_y = 7 - parity * 7

    def put(piece, x0, y0):
        nx, ny = piece.shape[:2]
        v = piece[...].reshape(nx * ny, 16, 256)
        even, odd = v[:, :, :128], v[:, :, 128:]
        where = (pl.ds(x0, nx), pl.ds(y0, ny))
        shape = (nx, ny, 16, 128)
        xc[where + (slice(None), slice(0, 128))] = shifted(odd, -1).reshape(shape)
        xc[where + (slice(None), slice(128, 256))] = even.reshape(shape)
        xc[where + (slice(None), slice(256, 384))] = odd.reshape(shape)
        xc[where + (slice(None), slice(384, 512))] = shifted(even, 1).reshape(shape)

    put(own, 3, 3)
    put(xm, 0, 3)
    put(xp, 7, 3)
    put(off, 0, off_y)
    put(pair, 0, pair_y)
    xc_out[...] = xc[2:8, 2:8]

    for plane in range(4):
        total = None
        for r in range(2):
            pre = None
            for a in range(3):
                lhs = jnp.concatenate(
                    [
                        xc[2 * plane + a : 2 * plane + a + 2, b : b + 8, :, r * 128 : r * 128 + 384].reshape(256, 384)
                        for b in range(3)
                    ],
                    axis=1,
                )
                part = nt(lhs, w1[:, a * 1152 : (a + 1) * 1152])
                pre = part if pre is None else pre + part
            pre = pre.reshape(2, 8, 16, 256)
            logistic = sigmoid(pre)
            if plane in (1, 2):
                inner, gate = pre[:, 2:6], logistic[:, 2:6]
                slope_out[r, 2 * plane - 2 : 2 * plane] = gate * (1.0 + inner * (1.0 - gate))
            value = (pre * logistic).reshape(2, 4, 2, 16, 256)
            value = (value[0, :, 0] + value[0, :, 1]) + (value[1, :, 0] + value[1, :, 1])
            total = value if total is None else total + value
        row = lax.broadcasted_iota(jnp.int32, total.shape, 0)
        keep = ((row > 0) | (filt_at > 0)) & ((row < 3) | (filt_at < 15))
        if plane == 0:
            keep = keep & (space_at > 0)
        if plane == 3:
            keep = keep & (space_at < 7)
        pooled_out[plane] = jnp.where(keep, total * 0.125, 0.0).astype(BF16)


def load_chunks(w2_hbm, w2, sem):
    loads = []
    for t in range(9):
        lanes = slice(t * 768, (t + 1) * 768)
        loads.append(pltpu.make_async_copy(w2_hbm.at[:, lanes], w2.at[:, lanes], sem.at[t]))
        loads[-1].start()
    return loads


def second_kernel_body(pooled, cot, w2_hbm, act_out, g2_out, pc, w2, sem):
    loads = load_chunks(w2_hbm, w2, sem)
    v = pooled[...].reshape(16, 16, 256)
    pc[:, :, :, 0:256] = shifted(v, -1).reshape(4, 4, 16, 256)
    pc[:, :, :, 256:512] = pooled[...]
    pc[:, :, :, 512:768] = shifted(v, 1).reshape(4, 4, 16, 256)
    pre = None
    for a in range(3):
        for b in range(3):
            t = 3 * a + b
            loads[t].wait()
            cells = pc[a : a + 2, b : b + 2].reshape(64, 768)
            part = nt(w2[:, t * 768 : (t + 1) * 768], cells)
            pre = part if pre is None else pre + part
    logistic = sigmoid(pre)
    act_out[...] = (pre * logistic).astype(act_out.dtype)
    grad = cot[...].astype(F32) * (logistic * (1.0 + pre * (1.0 - logistic)))
    g2_out[...] = jnp.transpose(grad).astype(BF16).reshape(2, 2, 16, 512)


def backward_kernel(own, xm, xp, off, pair, slope, xc, w2_hbm, keep_out, send_out, gc, w2, sem):
    loads = load_chunks(w2_hbm, w2, sem)
    parity = lax.rem(lax.axis_index("filt"), 2)
    off_y = parity * 3
    pair_y = 3 - parity * 3

    def put(piece, x0, y0):
        nx, ny = piece.shape[:2]
        v = piece[...].reshape(nx * ny, 16, 512)
        where = (pl.ds(x0, nx), pl.ds(y0, ny))
        shape = (nx, ny, 16, 512)
        gc[where + (slice(None), slice(0, 512))] = shifted(v, 1).reshape(shape)
        gc[where + (slice(None), slice(512, 1024))] = v.reshape(shape)
        gc[where + (slice(None), slice(1024, 1536))] = shifted(v, -1).reshape(shape)

    put(own, 1, 1)
    put(xm, 0, 1)
    put(xp, 3, 1)
    put(off, 0, off_y)
    put(pair, 0, pair_y)

    acc = None
    for a in range(3):
        for b in range(3):
            t = 3 * a + b
            loads[t].wait()
            for c in range(3):
                cells = gc[2 - a : 4 - a, 2 - b : 4 - b, :, c * 512 : (c + 1) * 512].reshape(64, 512)
                part = nn(cells, w2[:, (3 * t + c) * 256 : (3 * t + c + 1) * 256])
                acc = part if acc is None else acc + part
    acc = (acc * 0.125).reshape(2, 2, 16, 256)

    row = lax.broadcasted_iota(jnp.int32, (256, 256), 0)
    column = lax.broadcasted_iota(jnp.int32, (256, 256), 1)
    half = row // 128
    inside = row - half * 128
    want = 4 * (inside // 2) + lax.rem(inside, 2) + 2 * jnp.where(half == 0, parity, 1 - parity)
    order = jnp.where(column == want, 1.0, 0.0).astype(BF16)
    turned = []
    for r in range(2):
        grads = [
            (acc[x // 2, y // 2] * slope[r, x, y]).astype(BF16)
            for x in range(4)
            for y in range(4)
        ]
        turned.append(nt(order, jnp.concatenate(grads, axis=0)).astype(BF16))
    for a in range(3):
        for b in range(3):
            t = 3 * a + b
            part = None
            for r in range(2):
                cells = xc[a : a + 4, b : b + 4, :, r * 128 : r * 128 + 384].reshape(256, 384)
                one = nn(turned[r], cells)
                part = one if part is None else part + one
            part = part.astype(BF16)
            keep_out[:, t * 384 : (t + 1) * 384] = part[:128]
            send_out[:, t * 384 : (t + 1) * 384] = part[128:]


def route(step, across, spaces, filts):
    pairs = []
    for i in range(spaces):
        for j in range(filts):
            to_i = i + step
            to_j = (j + 1 if j % 2 else j - 1) if across else j
            if 0 <= to_i < spaces and 0 <= to_j < filts:
                pairs.append((i * filts + j, to_i * filts + to_j))
    return pairs


def surround(x, width, beside):
    spaces, filts = lax.axis_size("space"), lax.axis_size("filt")
    length = x.shape[1]
    parity = lax.rem(lax.axis_index("filt"), 2)
    far = parity * (length - width)
    near = (length - width) - far
    last, first = x[x.shape[0] - width :], x[:width]
    xm = lax.ppermute(last, BOTH, route(1, False, spaces, filts))
    xp = lax.ppermute(first, BOTH, route(-1, False, spaces, filts))
    xp, beside = lax.optimization_barrier((xp, beside))
    wide = jnp.concatenate([xm, x, xp], axis=0)
    off = lax.ppermute(lax.dynamic_slice_in_dim(wide, far, width, 1), BOTH, route(0, True, spaces, filts))
    pair = lax.ppermute(lax.dynamic_slice_in_dim(wide, near, width, 1), "filt", [(j, j ^ 1) for j in range(filts)])
    return (x, xm, xp, off, pair), beside


def steps(layer_input, first_kernel, second_kernel, cotangent):
    filts = lax.axis_size("filt")
    folded = layer_input.reshape(4, 4, 16, 256)
    cot = cotangent.reshape(32, 2, 16, 32).transpose(2, 0, 1, 3).reshape(16, 16, 128)
    pieces, cot = surround(folded, 3, cot)
    cot = lax.all_to_all(cot, "filt", 0, 0)
    cot = cot.reshape(512, 64)
    xc, slope, pooled = pl.pallas_call(
        first_kernel_body,
        out_shape=(
            jax.ShapeDtypeStruct((6, 6, 16, 512), BF16),
            jax.ShapeDtypeStruct((2, 4, 4, 16, 256), F32),
            jax.ShapeDtypeStruct((4, 4, 16, 256), BF16),
        ),
        in_specs=[VMEM] * 6,
        out_specs=(VMEM,) * 3,
        scratch_shapes=[pltpu.VMEM((10, 10, 16, 512), BF16)],
        compiler_params=pltpu.CompilerParams(vmem_limit_bytes=40 << 20),
        name="first_layer",
    )(*pieces, first_kernel)
    act, grad = pl.pallas_call(
        second_kernel_body,
        out_shape=(
            jax.ShapeDtypeStruct((512, 64), BF16),
            jax.ShapeDtypeStruct((2, 2, 16, 512), BF16),
        ),
        in_specs=[VMEM] * 2 + [HBM],
        out_specs=(VMEM,) * 2,
        scratch_shapes=[
            pltpu.VMEM((4, 4, 16, 768), BF16),
            pltpu.VMEM((512, 6912), BF16),
            pltpu.SemaphoreType.DMA((9,)),
        ],
        compiler_params=pltpu.CompilerParams(vmem_limit_bytes=48 << 20),
        name="second_layer",
    )(pooled, cot, second_kernel)
    grads, act = surround(grad, 1, act.reshape(16, 16, 128))
    keep, send = pl.pallas_call(
        backward_kernel,
        out_shape=(jax.ShapeDtypeStruct((128, 3456), BF16),) * 2,
        in_specs=[VMEM] * 7 + [HBM],
        out_specs=(VMEM,) * 2,
        scratch_shapes=[
            pltpu.VMEM((4, 4, 16, 1536), BF16),
            pltpu.VMEM((512, 6912), BF16),
            pltpu.SemaphoreType.DMA((9,)),
        ],
        compiler_params=pltpu.CompilerParams(vmem_limit_bytes=48 << 20),
        name="backward_layers",
    )(*grads, slope, xc, second_kernel)
    got = lax.ppermute(send, "filt", [(j, j ^ 1) for j in range(filts)])
    both = (keep.astype(F32) + got.astype(F32)).astype(BF16)
    spaces = lax.axis_size("space")
    groups = [[i * filts + j for i in range(spaces) for j in range(c, filts, 2)] for c in range(2)]
    parts = lax.all_to_all(both.reshape(64, 2, 3456), BOTH, 0, 0, axis_index_groups=groups)
    act = lax.all_to_all(act, "filt", 0, 0)
    activation = act.reshape(16, 32, 2, 32).transpose(1, 2, 0, 3).reshape(32, 2, 512).astype(F32)
    kernel_grad = parts.astype(F32).sum(axis=0)
    return (activation, kernel_grad)


def solution(mesh):
    return jax.shard_map(
        steps,
        mesh=mesh,
        in_specs=(P("space", "filt", None, None), P(), P(), P("filt", "space", None)),
        out_specs=(P("filt", "space", None), P(BOTH, None)),
        check_vma=False,
    )
```
